32 devices in a mesh: row: 4 (over z), col: 8 (over y, x, core).
Axes of the slice: x: 2, y: 2, z: 4, core: 2. Of those that a mesh axis runs over, the one named last changes fastest.
Arguments:
- dec_src: float32 [2304, 8192], P('col', 'row'), may hold values from -6 to 6
- enc_tgt: float32 [2304, 16384], P('row', 'col'), may hold values from -0.125 to 0.125
- src_coacts: float32 [512, 8192], P('col', 'row'), may hold values from -6 to 6
- tgt_coacts: float32 [512, 16384], P('row', 'col'), may hold values from -6 to 6
- eval_src: float32 [512, 8192], P('col', 'row'), may hold values from -6 to 6
- enc_bias: float32 [16384], P('col'), may hold values from -0.5 to 0.5
- dec_tgt: float32 [2304, 16384], P('row', 'col'), may hold values from -0.046875 to 0.046875
- tile_mask: int32 [128, 256], P('row', 'col'), may hold values from 0 to 1, as said below
Outputs:
- recon: float32 [512, 2304], P('col', 'row')
The draws below stay inside these ranges and needn't reach their ends.
Inputs may be any that keep to these rules, and one draw needn't show every extreme that they name: `tile_mask`: 1 keeps a tile, 0 prunes it; the share of kept tiles differs between regions of the grid.
All inputs are finite; a program needn't handle non-finite values.
Results may differ from the reference program's by a relative error of at most 0.0003.
Values sent between devices are 32-bit elements; how exact they have to be, the bound alone decides.
A program may use at most 192 MiB of HBM per device.

```python
import jax
import jax.numpy as jnp
from jax import lax

D = 2304
T_SIZE = 16384
S = 8192
TILE = 64
NG = 512
E = 512
N_ROW = 4


def draw_tile_mask(key, part):
    block_rows = jnp.arange(S // TILE, dtype=jnp.int32)[:, None]
    block_cols = jnp.arange(T_SIZE // TILE, dtype=jnp.int32)[None, :]
    level = block_rows * 8 // (S // TILE) + block_cols * 8 // (T_SIZE // TILE)
    percent = 15 + level * 5
    rolled = jax.random.randint(jax.random.fold_in(key, 11), (S // TILE, T_SIZE // TILE), 0, 100, dtype=jnp.int32)
    return (rolled < percent).astype(jnp.int32)


def levels(rng, shape, shards, low, top_value):
    def one(position, shards_of):
        draws = jax.random.uniform(jax.random.fold_in(jax.random.fold_in(rng, 6), position), (shards_of,), jnp.float32, low / len(shards), top_value / len(shards))
        return jnp.repeat(jnp.exp(draws), shape[position] // shards_of).reshape((-1,) + (1,) * (len(shape) - position - 1))

    gain = one(*shards[0])
    for cut in shards[1:]:
        gain = gain * one(*cut)
    return gain


def centred(key, shape, scale, reach, pieces=(), kind=jnp.bfloat16):
    factor_of = levels(key, shape, pieces, -0.22, 0.18) if pieces else 1.0
    drawn = jax.random.normal(key, shape, jnp.float32) * scale * factor_of
    return jnp.minimum(jnp.maximum(drawn, -reach), reach).astype(kind)


def setup_inputs(seed: int = 0) -> dict:
    key_of = jax.random.split(jax.random.key(seed), 9)
    return {
        "dec_src": centred(key_of[0], (D, S), 1.0, 6.0, ((0, 8), (1, 4)), jnp.float32),
        "enc_tgt": centred(key_of[1], (D, T_SIZE), D ** -0.5, 0.125, ((0, 4), (1, 8)), jnp.float32),
        "src_coacts": centred(key_of[2], (NG, S), 1.0, 6.0, ((0, 8), (1, 4)), jnp.float32),
        "tgt_coacts": centred(key_of[3], (NG, T_SIZE), 1.0, 6.0, ((0, 4), (1, 8)), jnp.float32),
        "eval_src": centred(key_of[4], (E, S), 1.0, 6.0, ((0, 8), (1, 4)), jnp.float32),
        "enc_bias": jnp.clip(jax.random.uniform(key_of[5], (T_SIZE,), jnp.float32, -0.5, 0.5) * levels(key_of[5], (T_SIZE,), ((0, 8),), -0.4, 0.0), -0.5, 0.5),
        "dec_tgt": centred(key_of[6], (D, T_SIZE), T_SIZE ** -0.5, 0.046875, ((0, 4), (1, 8)), jnp.float32),
        "tile_mask": draw_tile_mask(jax.random.fold_in(key_of[8], 71), 0),
    }


PRECISE = lax.Precision.HIGHEST

def reference(dec_src, enc_tgt, src_coacts, tgt_coacts, eval_src, enc_bias, dec_tgt, tile_mask):
    block_rows = S // N_ROW
    tile_rows = block_rows // TILE
    tile_cols = T_SIZE // TILE
    norm_gram = 1.0 / jnp.sqrt(jnp.float32(NG))

    def accumulate(pre_acts, block_index):
        offset = (block_index * block_rows).astype(jnp.int32)
        dec_block = lax.dynamic_slice_in_dim(dec_src, offset, block_rows, 1)
        virtual = lax.dot_general(dec_block, enc_tgt, (((0,), (0,)), ((), ())), precision=PRECISE, preferred_element_type=jnp.float32)
        src_block = lax.dynamic_slice_in_dim(src_coacts, offset, block_rows, 1)
        coact = lax.dot_general(src_block, tgt_coacts, (((0,), (0,)), ((), ())), precision=PRECISE, preferred_element_type=jnp.float32) * norm_gram
        mask_block = lax.dynamic_slice_in_dim(tile_mask, (block_index * tile_rows).astype(jnp.int32), tile_rows, 0).astype(jnp.float32)
        weighted = ((virtual * coact).reshape(tile_rows, TILE, tile_cols, TILE) * mask_block[:, None, :, None]).reshape(block_rows, T_SIZE)
        eval_block = lax.dynamic_slice_in_dim(eval_src, offset, block_rows, 1)
        return (pre_acts + jnp.dot(eval_block, weighted, precision=PRECISE, preferred_element_type=jnp.float32), None)
    pre_acts, _ = lax.scan(accumulate, jnp.zeros((E, T_SIZE), jnp.float32), jnp.arange(N_ROW, dtype=jnp.int32))
    hidden = jnp.maximum(pre_acts / jnp.sqrt(jnp.float32(S)) + enc_bias[None, :], 0.0)
    return lax.dot_general(hidden, dec_tgt, (((1,), (1,)), ((), ())), precision=PRECISE, preferred_element_type=jnp.float32)
```

```python
import functools

import jax
import jax.numpy as jnp
from jax import lax
from jax.experimental import pallas as pl
from jax.experimental.pallas import tpu as pltpu
from jax.sharding import PartitionSpec as P


CHUNKS = 2


def split(value):
    high = value.astype(jnp.bfloat16)
    return high, (value - high.astype(jnp.float32)).astype(jnp.bfloat16)


def dot3(left, rows, right, left_dim, right_dim):
    def one(a, b):
        return lax.dot_general(a, b, (((left_dim,), (right_dim,)), ((), ())), preferred_element_type=jnp.float32)

    both = one(left, right[0])
    return both[:rows] + (both[rows:] + one(left[:rows], right[1]))


def prepare(enc_rows, row, *refs):
    blocks, (enc_both, tgt_both, ordered) = refs[:-3], refs[-3:]
    n_row, height = len(blocks), ordered.shape[2]
    for step, block in enumerate(blocks):
        ordered[lax.rem(row[0] + n_row - step, n_row)] = block[...]
    for rows, out in ((slice(None, enc_rows), enc_both), (slice(enc_rows, None), tgt_both)):
        out[:height], out[height:] = split(ordered[:, rows, :].reshape(-1, height).T)


def prepare_target(row, blocks, enc_rows):
    n_row = len(blocks)
    rows, height = blocks[0].shape
    shapes = [(2 * height, n_row * n) for n in (enc_rows, rows - enc_rows)]
    return pl.pallas_call(
        functools.partial(prepare, enc_rows),
        in_specs=[pl.BlockSpec(memory_space=pltpu.SMEM)] + [pl.BlockSpec(memory_space=pltpu.VMEM)] * n_row,
        out_specs=[pl.BlockSpec(memory_space=pltpu.VMEM)] * 2,
        out_shape=[jax.ShapeDtypeStruct(shape, jnp.bfloat16) for shape in shapes],
        scratch_shapes=[pltpu.VMEM((n_row, rows, height), jnp.float32)],
        compiler_params=pltpu.CompilerParams(vmem_limit_bytes=60 * 1024 * 1024),
        cost_estimate=pl.CostEstimate(flops=0, bytes_accessed=8 * n_row * rows * height, transcendentals=0),
    )(row.reshape(1), *blocks)


def weigh(dec_rows, src_rows, norm, source, enc_both, tgt_both, mask, out):
    width = source.shape[2]
    height = out.shape[0]

    @pl.when(pl.program_id(0) == 0)
    def _():
        out[...] = jnp.zeros_like(out)

    dec = split(source[:, :dec_rows, :].reshape(-1, width))
    virtual = dot3(enc_both[...], height, dec, 1, 0)
    src = split(source[:, dec_rows : dec_rows + src_rows, :].reshape(-1, width))
    coact = dot3(tgt_both[...], height, src, 1, 0) * norm
    tiles = mask.shape[1]
    keep = jnp.broadcast_to(mask[0][:, None, :], (tiles, height // tiles, width)).reshape(height, width)
    weighted = jnp.concatenate(split(virtual * coact * keep), axis=0)
    evals = split(source[:, dec_rows + src_rows :, :].reshape(-1, width))
    out[...] += dot3(weighted, height, evals, 1, 1)


def partial_pre(source, target, mask, dec_rows, src_rows, norm):
    n_col, packed, count = source.shape
    height = target[0].shape[0] // 2
    depth, stats = target[0].shape[1], target[1].shape[1]
    width = min(256, count)
    evals = n_col * (packed - dec_rows - src_rows)
    return pl.pallas_call(
        functools.partial(weigh, dec_rows, src_rows, norm),
        grid=(count // width,),
        in_specs=[
            pl.BlockSpec((n_col, packed, width), lambda i: (0, 0, i)),
            pl.BlockSpec(target[0].shape, lambda i: (0, 0)),
            pl.BlockSpec(target[1].shape, lambda i: (0, 0)),
            pl.BlockSpec((1, mask.shape[1], width), lambda i: (0, 0, i)),
        ],
        out_specs=pl.BlockSpec((height, evals), lambda i: (0, 0)),
        out_shape=jax.ShapeDtypeStruct((height, evals), jnp.float32),
        compiler_params=pltpu.CompilerParams(vmem_limit_bytes=60 * 1024 * 1024),
        cost_estimate=pl.CostEstimate(
            flops=6 * count * height * (depth + stats + evals),
            bytes_accessed=4 * (source.size + height * (depth + stats)),
            transcendentals=0,
        ),
    )(source, *target, mask)


def layer(n_row, dec_src, enc_tgt, src_coacts, tgt_coacts, eval_src, enc_bias, dec_tgt, tile_mask):
    members = n_row // 2
    src_count = dec_src.shape[1]
    half = enc_tgt.shape[1] // 2
    chunk = half // CHUNKS
    piece = chunk // members
    dec_rows, src_rows, enc_rows = dec_src.shape[0], src_coacts.shape[0], enc_tgt.shape[0]
    stats = tgt_coacts.shape[0] * n_row
    tile = src_count // tile_mask.shape[0]
    row = lax.axis_index("row")
    parity = lax.rem(row, 2)
    group = row // 2
    norm = 1.0 / float(stats) ** 0.5

    packed = jnp.concatenate([dec_src, src_coacts, eval_src], axis=0)
    packed_other = lax.ppermute(packed, "row", [(r, r ^ 1) for r in range(n_row)])
    mask_t = tile_mask.T.astype(jnp.float32)
    mask_here = lax.dynamic_slice_in_dim(mask_t, parity * (half // tile), half // tile, 0)
    mask_there = lax.dynamic_slice_in_dim(mask_t, (1 - parity) * (half // tile), half // tile, 0)
    mask_other = lax.ppermute(mask_there, "row", [(r, r ^ 1) for r in range(n_row)])

    sources = [(lax.all_gather(packed, "col", axis=0, tiled=False), jnp.repeat(mask_here, tile, axis=1))]
    gathered = lax.all_gather(packed_other, "col", axis=0, tiled=False)
    sources.append((gathered, jnp.repeat(mask_other, tile, axis=1)))

    targets = []
    for k in range(CHUNKS):
        def columns(side):
            start = side * half + k * chunk
            return jnp.concatenate(
                [lax.dynamic_slice_in_dim(a, start, chunk, 1) for a in (enc_tgt, tgt_coacts)], axis=0
            )

        same, across = columns(parity), columns(1 - parity)
        blocks = []
        for step in range(n_row):
            block = same if step % 2 == 0 else across
            if step:
                block = lax.ppermute(block, "row", [(r, (r + step) % n_row) for r in range(n_row)])
            blocks.append(block)
        targets.append(prepare_target(row, blocks, enc_rows))

    scale = 1.0 / jnp.sqrt(jnp.float32(src_count * n_row))
    recon_part = None
    for k in range(CHUNKS):
        partial = None
        for gathered, mask in sources:
            rows = chunk // tile
            term = partial_pre(gathered, targets[k], mask[None, k * rows : (k + 1) * rows], dec_rows, src_rows, norm)
            partial = term if partial is None else partial + term
        total = lax.dynamic_slice_in_dim(partial, group * piece, piece, 0)
        for step in range(1, members):
            target = lax.rem(group + step, members)
            sent = lax.dynamic_slice_in_dim(partial, target * piece, piece, 0)
            arrived = lax.ppermute(sent, "row", [(r, (r + 2 * step) % n_row) for r in range(n_row)])
            total = total + arrived
        bias = lax.dynamic_slice_in_dim(enc_bias, parity * half + k * chunk + group * piece, piece, 0)
        hidden = jnp.maximum(total * scale + bias[:, None], 0.0)
        hidden_all = lax.all_gather(hidden, "row", axis=0, tiled=True)
        starts = [(r % 2) * half + k * chunk + (r // 2) * piece for r in range(n_row)]
        dec_part = jnp.concatenate([dec_tgt[:, s : s + piece] for s in starts], axis=1)
        term = lax.dot_general(
            hidden_all, dec_part, (((0,), (1,)), ((), ())),
            precision=lax.Precision.HIGH, preferred_element_type=jnp.float32,
        )
        recon_part = term if recon_part is None else recon_part + term
    return lax.psum_scatter(recon_part, "col", scatter_dimension=0, tiled=True)


MESH = pl.DeviceIdType.MESH
T_CHUNKS = 4
S_CHUNKS = 4
X, Y, CORE = 2, 4, 1
HOPS = (
    (0, "all", X), (0, "all", Y), (0, "all", CORE),
    (X, "all", CORE), (Y, "all", CORE),
    (X, "top", Y), (Y, "low", X),
    (X ^ Y, "top", CORE), (X ^ Y, "low", CORE),
)


def fused(sizes, packed, blocks, masks, bias, dec_tgt, out, sbuf, tbuf, *scratch):
    n_row, n_col, dec_rows, src_rows, enc_rows, norm, scale = sizes
    (tstage, encs, tgts, stage, mask, acc, arrived, hidden, decoder, recon, rsend, rrecv,
     t_send, t_recv, s_send, s_recv, m_send, m_recv, x_send, x_recv, p_send, p_recv, h_send, h_recv,
     r_send, r_recv, local_sem, load_sem) = scratch
    r, c = lax.axis_index("row"), lax.axis_index("col")
    parity = lax.rem(r, 2)
    count = packed.shape[1]
    jw = count // S_CHUNKS
    half = blocks.shape[1] // 2
    w = half // T_CHUNKS
    packed_rows = packed.shape[0]
    width = min(256, jw)

    def row_of(step):
        return lax.rem(r + step, n_row)

    def remote(src, dst, send, recv, row, col):
        return pltpu.make_async_remote_copy(
            src_ref=src, dst_ref=dst, send_sem=send, recv_sem=recv, device_id=(row, col), device_id_type=MESH
        )

    def t_cols(side, k):
        return pl.ds(pl.multiple_of(side * half + k * w, w), w)

    def t_copy(k, step):
        to = row_of(step)
        return remote(
            blocks.at[:, t_cols(lax.rem(to, 2), k)], tbuf.at[k, r], t_send.at[k, step - 1], t_recv.at[k, step - 1], to, c
        )

    def t_wait(k, step):
        slot = tbuf.at[k, row_of(n_row - step)]
        remote(slot, slot, t_send.at[k, step - 1], t_recv.at[k, step - 1], row_of(step), c).wait_recv()

    def s_cols(j):
        return pl.ds(pl.multiple_of(j * jw, jw), jw)

    def s_copy(j):
        return remote(packed.at[:, s_cols(j)], sbuf.at[1, c, :, s_cols(j)], s_send.at[j], s_recv.at[j], r ^ 1, c)

    def m_copy():
        return remote(masks.at[1 - parity], mask.at[1], m_send, m_recv, r ^ 1, c)

    parts = {
        "all": pl.ds(0, packed_rows),
        "top": pl.ds(0, packed_rows // 2),
        "low": pl.ds(packed_rows // 2, packed_rows - packed_rows // 2),
    }

    def hop(q, n):
        whose, rows, to = HOPS[n]
        block, j = q // S_CHUNKS, q % S_CHUNKS
        dst = sbuf.at[block, c ^ whose, parts[rows], s_cols(j)]
        src = packed.at[parts[rows], s_cols(j)] if whose == 0 and block == 0 else dst
        return remote(src, dst, x_send.at[q, n], x_recv.at[q, n], r, c ^ to)

    def hop_wait(q, n):
        whose, rows, to = HOPS[n]
        block, j = q // S_CHUNKS, q % S_CHUNKS
        dst = sbuf.at[block, c ^ whose ^ to, parts[rows], s_cols(j)]
        remote(dst, dst, x_send.at[q, n], x_recv.at[q, n], r, c ^ to).wait_recv()

    chunks = 2 * S_CHUNKS

    def spread(q):
        if q >= S_CHUNKS:
            s_copy(q - S_CHUNKS).wait_recv()
        for n in (0, 1, 2):
            hop(q, n).start()

    def step(q):
        if q < chunks:
            hop_wait(q, 0)
            hop(q, 5).start()
            hop(q, 3).start()
            hop_wait(q, 1)
            hop(q, 6).start()
            hop(q, 4).start()
        if q + 2 < chunks:
            spread(q + 2)
        if q >= 1:
            hop_wait(q - 1, 5)
            hop(q - 1, 7).start()
            hop_wait(q - 1, 6)
            hop(q - 1, 8).start()

    def landed(q):
        for n in (2, 3, 4, 7, 8):
            hop_wait(q, n)

    def load_copies(block, j, slot):
        copies = []
        for i in range(n_col):
            s = c ^ i
            copies.append(
                pltpu.make_async_copy(sbuf.at[block, s, :, s_cols(j)], stage.at[slot, s], load_sem.at[slot, i])
            )
        own = pltpu.make_async_copy(packed.at[:, s_cols(j)], stage.at[slot, c], load_sem.at[slot, 0])
        return copies, own

    def load_start(block, j, slot):
        copies, own = load_copies(block, j, slot)

        @pl.when(block == 0)
        def _():
            own.start()

        @pl.when(block != 0)
        def _():
            copies[0].start()

        for copy in copies[1:]:
            copy.start()

    def load_wait(slot):
        for i in range(n_col):
            s = c ^ i
            pltpu.make_async_copy(packed.at[:, s_cols(0)], stage.at[slot, s], load_sem.at[slot, i]).wait()

    def prepare_chunk(k):
        for s in range(1, n_row):
            t_wait(k, s)
        own = pltpu.make_async_copy(blocks.at[:, t_cols(parity, k)], tstage.at[r], local_sem.at[0])
        others = [
            pltpu.make_async_copy(tbuf.at[k, row_of(s)], tstage.at[row_of(s)], local_sem.at[s]) for s in range(1, n_row)
        ]
        for copy in [own] + others:
            copy.start()
        for copy in [own] + others:
            copy.wait()
        for rows, into in ((slice(None, enc_rows), encs), (slice(enc_rows, None), tgts)):
            into[k, :w], into[k, w:] = split(tstage[:, rows, :].reshape(-1, w).T)

    def compute(k, block, j, slot):
        @pl.loop(0, jw // width)
        def _(i):
            lanes = pl.ds(pl.multiple_of(i * width, width), width)
            dec = split(stage[slot, :, :dec_rows, lanes].reshape(-1, width))
            virtual = dot3(encs[k], w, dec, 1, 0)
            src = split(stage[slot, :, dec_rows : dec_rows + src_rows, lanes].reshape(-1, width))
            coact = dot3(tgts[k], w, src, 1, 0) * norm
            keep = mask[block, k, :, pl.ds(pl.multiple_of(j * jw + i * width, width), width)]
            tiles = keep.shape[0]
            keep = jnp.broadcast_to(keep[:, None, :], (tiles, w // tiles, width)).reshape(w, width)
            weighted = jnp.concatenate(split(virtual * coact * keep), axis=0)
            evals = split(stage[slot, :, dec_rows + src_rows :, lanes].reshape(-1, width))
            acc[k] += dot3(weighted, w, evals, 1, 1)

    def p_copy(k):
        return remote(acc.at[k], arrived.at[k], p_send.at[k], p_recv.at[k], r ^ 2, c)

    def h_copy(k, side):
        return remote(hidden.at[side, k], hidden.at[side, k], h_send.at[k], h_recv.at[k], r ^ 1, c)

    def activate(k):
        p_copy(k).wait_recv()
        column = bias[pl.ds(pl.multiple_of(parity * half + k * w, w), w), :]
        hidden[parity, k] = jnp.maximum((acc[k] + arrived[k]) * scale + column, 0.0)
        h_copy(k, parity).start()

    def decode(k):
        h_copy(k, 1 - parity).wait_recv()
        for side in range(2):
            left = jnp.concatenate(split(decoder[:, t_cols(side, k)]), axis=0)
            recon[...] += dot3(left, decoder.shape[0], split(hidden[side, k]), 1, 0)

    def scatter_copy(i):
        rows = rsend.shape[0] // n_col
        there = c ^ i
        return remote(
            rsend.at[pl.ds(pl.multiple_of(there * rows, rows), rows)], rrecv.at[c], r_send.at[i - 1], r_recv.at[i - 1], r, there
        )

    def scatter_wait(i):
        remote(rrecv.at[c ^ i], rrecv.at[c ^ i], r_send.at[i - 1], r_recv.at[i - 1], r, c ^ i).wait_recv()

    barrier = pltpu.get_barrier_semaphore()
    for s in range(1, n_row):
        pl.semaphore_signal(barrier, inc=1, device_id=(row_of(s), c), device_id_type=MESH)
    for i in range(1, n_col):
        pl.semaphore_signal(barrier, inc=1, device_id=(r, c ^ i), device_id_type=MESH)
    pl.semaphore_wait(barrier, n_row + n_col - 2)

    m_copy().start()
    for s in range(1, n_row):
        t_copy(0, s).start()
    spread(0)
    for j in range(S_CHUNKS):
        s_copy(j).start()
    spread(1)
    for k in range(1, T_CHUNKS):
        for s in range(1, n_row):
            t_copy(k, s).start()
    own_mask = pltpu.make_async_copy(masks.at[parity], mask.at[0], local_sem.at[n_row])
    own_mask.start()
    own_decoder = pltpu.make_async_copy(dec_tgt, decoder, local_sem.at[n_row + 1])
    own_decoder.start()
    acc[...] = jnp.zeros_like(acc)
    recon[...] = jnp.zeros_like(recon)
    step(0)
    step(1)
    own_mask.wait()
    own_decoder.wait()
    m_copy().wait_recv()

    def where(g):
        k = jnp.where(g < 6, 0, jnp.where(g < 12, 1, jnp.where(g < 16, g % 2, g // 8)))
        block = jnp.where(
            g < 4, 0, jnp.where(g < 6, 1, jnp.where(g < 10, 0, jnp.where(g < 16, 1, (g // 4) % 2)))
        )
        j = jnp.where(
            g < 4, g, jnp.where(g < 6, g - 4, jnp.where(g < 10, g - 6, jnp.where(g < 12, g - 10, jnp.where(g < 16, 2 + (g - 12) // 2, g % 4))))
        )
        return k, block, j

    needs = {0: 0, 1: 1, 2: 2, 3: 3, 4: 4, 5: 5, 12: 6, 14: 7}
    steps = {1: 2, 2: 3, 3: 4, 4: 5, 5: 6, 12: 7, 14: 8}

    @pl.loop(0, T_CHUNKS * chunks)
    def _(g):
        k, block, j = where(g)
        slot = g % 2
        for at, q in needs.items():
            @pl.when(g == at)
            def _(at=at, q=q):
                if at in steps:
                    step(steps[at])
                landed(q)

        waits = functools.reduce(jnp.logical_or, [g == at for at in needs])
        next_waits = functools.reduce(jnp.logical_or, [g + 1 == at for at in needs])

        @pl.when(waits)
        def _():
            load_start(block, j, slot)

        @pl.when((g == 0) | (g == 6) | (g == 16) | (g == 24))
        def _():
            prepare_chunk(k)

        @pl.when(jnp.logical_not(next_waits) & (g + 1 < T_CHUNKS * chunks))
        def _():
            load_start(*where(g + 1)[1:], 1 - slot)

        load_wait(slot)
        compute(k, block, j, slot)

        @pl.when((g == 14) | (g == 15) | (g == 23) | (g == 31))
        def _():
            p_copy(k).start()

        @pl.when((g == 27) | (g == 28) | (g == 30))
        def _():
            activate(jnp.where(g == 30, 2, g - 27))

    for k in range(T_CHUNKS):
        if k == T_CHUNKS - 1:
            activate(k)
        decode(k)
    rsend[...] = recon[...].T
    for i in range(1, n_col):
        scatter_copy(i).start()
    rows = rsend.shape[0] // n_col
    for i in range(1, n_col):
        scatter_wait(i)
    total = rsend[pl.ds(pl.multiple_of(c * rows, rows), rows), :]
    for i in range(1, n_col):
        total = total + rrecv[c ^ i]
    out[...] = total

    m_copy().wait_send()
    for j in range(S_CHUNKS):
        s_copy(j).wait_send()
    for k in range(T_CHUNKS):
        for s in range(1, n_row):
            t_copy(k, s).wait_send()
        p_copy(k).wait_send()
        h_copy(k, parity).wait_send()
    for q in range(chunks):
        for n in range(len(HOPS)):
            hop(q, n).wait_send()
    for i in range(1, n_col):
        scatter_copy(i).wait_send()


def whole(n_row, n_col, dec_src, enc_tgt, src_coacts, tgt_coacts, eval_src, enc_bias, dec_tgt, tile_mask):
    count, features = dec_src.shape[1], enc_tgt.shape[1]
    dec_rows, src_rows, ev_rows = dec_src.shape[0], src_coacts.shape[0], eval_src.shape[0]
    enc_rows, tgt_rows = enc_tgt.shape[0], tgt_coacts.shape[0]
    half = features // 2
    w = half // T_CHUNKS
    jw = count // S_CHUNKS
    packed = jnp.concatenate([dec_src, src_coacts, eval_src], axis=0)
    blocks = jnp.concatenate([enc_tgt, tgt_coacts], axis=0)
    tile = count // tile_mask.shape[0]
    masks = jnp.repeat(tile_mask.T.astype(jnp.float32), tile, axis=1).reshape(2, T_CHUNKS, w // tile, count)
    sizes = (
        n_row, n_col, dec_rows, src_rows, enc_rows,
        1.0 / float(tgt_rows * n_row) ** 0.5, 1.0 / float(count * n_row) ** 0.5,
    )
    evals = ev_rows * n_col
    depth, stats = dec_rows * n_col, src_rows * n_col
    anywhere, vmem = pl.BlockSpec(memory_space=pl.ANY), pl.BlockSpec(memory_space=pltpu.VMEM)
    dma = pltpu.SemaphoreType.DMA
    f32, bf16 = jnp.float32, jnp.bfloat16
    hops = (2 * S_CHUNKS, len(HOPS))
    outs = pl.pallas_call(
        functools.partial(fused, sizes),
        in_specs=[anywhere, anywhere, anywhere, vmem, anywhere],
        out_specs=[vmem, anywhere, anywhere],
        out_shape=[
            jax.ShapeDtypeStruct((ev_rows, dec_tgt.shape[0]), f32),
            jax.ShapeDtypeStruct((2, n_col, packed.shape[0], count), f32),
            jax.ShapeDtypeStruct((T_CHUNKS, n_row, blocks.shape[0], w), f32),
        ],
        scratch_shapes=[
            pltpu.VMEM((n_row, blocks.shape[0], w), f32),
            pltpu.VMEM((T_CHUNKS, 2 * w, depth), bf16),
            pltpu.VMEM((T_CHUNKS, 2 * w, stats), bf16),
            pltpu.VMEM((2, n_col, packed.shape[0], jw), f32),
            pltpu.VMEM((2,) + masks.shape[1:], f32),
            pltpu.VMEM((T_CHUNKS, w, evals), f32),
            pltpu.VMEM((T_CHUNKS, w, evals), f32),
            pltpu.VMEM((2, T_CHUNKS, w, evals), f32),
            pltpu.VMEM(dec_tgt.shape, f32),
            pltpu.VMEM((dec_tgt.shape[0], evals), f32),
            pltpu.VMEM((evals, dec_tgt.shape[0]), f32),
            pltpu.VMEM((n_col, ev_rows, dec_tgt.shape[0]), f32),
            dma((T_CHUNKS, n_row - 1)), dma((T_CHUNKS, n_row - 1)),
            dma((S_CHUNKS,)), dma((S_CHUNKS,)),
            dma(()), dma(()),
            dma(hops), dma(hops),
            dma((T_CHUNKS,)), dma((T_CHUNKS,)),
            dma((T_CHUNKS,)), dma((T_CHUNKS,)),
            dma((n_col - 1,)), dma((n_col - 1,)),
            dma((n_row + 2,)), dma((2, n_col)),
        ],
        compiler_params=pltpu.CompilerParams(
            collective_id=0, has_side_effects=True, vmem_limit_bytes=VMEM_LIMIT
        ),
    )(packed, blocks, masks, enc_bias.reshape(-1, 1), dec_tgt)
    return outs[0]


VMEM_LIMIT = 67000000


def solution(mesh):
    n_row, n_col = mesh.shape["row"], mesh.shape["col"]
    if (n_row, n_col) == (4, 8):
        return jax.shard_map(
            functools.partial(whole, n_row, n_col), mesh=mesh, in_specs=SPECS, out_specs=P("col", "row"), check_vma=False
        )
    return stepwise(mesh)


SPECS = (
    P("col", "row"), P("row", "col"), P("col", "row"), P("row", "col"),
    P("col", "row"), P("col"), P("row", "col"), P("row", "col"),
)


def stepwise(mesh):
    return jax.shard_map(
        functools.partial(layer, mesh.shape["row"]),
        mesh=mesh,
        in_specs=(
            P("col", "row"),
            P("row", "col"),
            P("col", "row"),
            P("row", "col"),
            P("col", "row"),
            P("col"),
            P("row", "col"),
            P("row", "col"),
        ),
        out_specs=P("col", "row"),
        check_vma=False,
    )
```

```python
import functools

import jax
import jax.numpy as jnp
from jax import lax
from jax.experimental import pallas as pl
from jax.experimental.pallas import tpu as pltpu
from jax.sharding import PartitionSpec as P


CHUNKS = 2


def split(value):
    high = value.astype(jnp.bfloat16)
    return high, (value - high.astype(jnp.float32)).astype(jnp.bfloat16)


def dot3(left, rows, right, left_dim, right_dim):
    def one(a, b):
        return lax.dot_general(a, b, (((left_dim,), (right_dim,)), ((), ())), preferred_element_type=jnp.float32)

    both = one(left, right[0])
    return both[:rows] + (both[rows:] + one(left[:rows], right[1]))


def prepare(enc_rows, row, *refs):
    blocks, (enc_both, tgt_both, ordered) = refs[:-3], refs[-3:]
    n_row, height = len(blocks), ordered.shape[2]
    for step, block in enumerate(blocks):
        ordered[lax.rem(row[0] + n_row - step, n_row)] = block[...]
    for rows, out in ((slice(None, enc_rows), enc_both), (slice(enc_rows, None), tgt_both)):
        out[:height], out[height:] = split(ordered[:, rows, :].reshape(-1, height).T)


def prepare_target(row, blocks, enc_rows):
    n_row = len(blocks)
    rows, height = blocks[0].shape
    shapes = [(2 * height, n_row * n) for n in (enc_rows, rows - enc_rows)]
    return pl.pallas_call(
        functools.partial(prepare, enc_rows),
        in_specs=[pl.BlockSpec(memory_space=pltpu.SMEM)] + [pl.BlockSpec(memory_space=pltpu.VMEM)] * n_row,
        out_specs=[pl.BlockSpec(memory_space=pltpu.VMEM)] * 2,
        out_shape=[jax.ShapeDtypeStruct(shape, jnp.bfloat16) for shape in shapes],
        scratch_shapes=[pltpu.VMEM((n_row, rows, height), jnp.float32)],
        compiler_params=pltpu.CompilerParams(vmem_limit_bytes=60 * 1024 * 1024),
        cost_estimate=pl.CostEstimate(flops=0, bytes_accessed=8 * n_row * rows * height, transcendentals=0),
    )(row.reshape(1), *blocks)


def weigh(dec_rows, src_rows, norm, source, enc_both, tgt_both, mask, out):
    width = source.shape[2]
    height = out.shape[0]

    @pl.when(pl.program_id(0) == 0)
    def _():
        out[...] = jnp.zeros_like(out)

    dec = split(source[:, :dec_rows, :].reshape(-1, width))
    virtual = dot3(enc_both[...], height, dec, 1, 0)
    src = split(source[:, dec_rows : dec_rows + src_rows, :].reshape(-1, width))
    coact = dot3(tgt_both[...], height, src, 1, 0) * norm
    tiles = mask.shape[1]
    keep = jnp.broadcast_to(mask[0][:, None, :], (tiles, height // tiles, width)).reshape(height, width)
    weighted = jnp.concatenate(split(virtual * coact * keep), axis=0)
    evals = split(source[:, dec_rows + src_rows :, :].reshape(-1, width))
    out[...] += dot3(weighted, height, evals, 1, 1)


def partial_pre(source, target, mask, dec_rows, src_rows, norm):
    n_col, packed, count = source.shape
    height = target[0].shape[0] // 2
    depth, stats = target[0].shape[1], target[1].shape[1]
    width = min(256, count)
    evals = n_col * (packed - dec_rows - src_rows)
    return pl.pallas_call(
        functools.partial(weigh, dec_rows, src_rows, norm),
        grid=(count // width,),
        in_specs=[
            pl.BlockSpec((n_col, packed, width), lambda i: (0, 0, i)),
            pl.BlockSpec(target[0].shape, lambda i: (0, 0)),
            pl.BlockSpec(target[1].shape, lambda i: (0, 0)),
            pl.BlockSpec((1, mask.shape[1], width), lambda i: (0, 0, i)),
        ],
        out_specs=pl.BlockSpec((height, evals), lambda i: (0, 0)),
        out_shape=jax.ShapeDtypeStruct((height, evals), jnp.float32),
        compiler_params=pltpu.CompilerParams(vmem_limit_bytes=60 * 1024 * 1024),
        cost_estimate=pl.CostEstimate(
            flops=6 * count * height * (depth + stats + evals),
            bytes_accessed=4 * (source.size + height * (depth + stats)),
            transcendentals=0,
        ),
    )(source, *target, mask)


def layer(n_row, dec_src, enc_tgt, src_coacts, tgt_coacts, eval_src, enc_bias, dec_tgt, tile_mask):
    members = n_row // 2
    src_count = dec_src.shape[1]
    half = enc_tgt.shape[1] // 2
    chunk = half // CHUNKS
    piece = chunk // members
    dec_rows, src_rows, enc_rows = dec_src.shape[0], src_coacts.shape[0], enc_tgt.shape[0]
    stats = tgt_coacts.shape[0] * n_row
    tile = src_count // tile_mask.shape[0]
    row = lax.axis_index("row")
    parity = lax.rem(row, 2)
    group = row // 2
    norm = 1.0 / float(stats) ** 0.5

    packed = jnp.concatenate([dec_src, src_coacts, eval_src], axis=0)
    packed_other = lax.ppermute(packed, "row", [(r, r ^ 1) for r in range(n_row)])
    mask_t = tile_mask.T.astype(jnp.float32)
    mask_here = lax.dynamic_slice_in_dim(mask_t, parity * (half // tile), half // tile, 0)
    mask_there = lax.dynamic_slice_in_dim(mask_t, (1 - parity) * (half // tile), half // tile, 0)
    mask_other = lax.ppermute(mask_there, "row", [(r, r ^ 1) for r in range(n_row)])

    sources = [(lax.all_gather(packed, "col", axis=0, tiled=False), jnp.repeat(mask_here, tile, axis=1))]
    gathered = lax.all_gather(packed_other, "col", axis=0, tiled=False)
    sources.append((gathered, jnp.repeat(mask_other, tile, axis=1)))

    targets = []
    for k in range(CHUNKS):
        def columns(side):
            start = side * half + k * chunk
            return jnp.concatenate(
                [lax.dynamic_slice_in_dim(a, start, chunk, 1) for a in (enc_tgt, tgt_coacts)], axis=0
            )

        same, across = columns(parity), columns(1 - parity)
        blocks = []
        for step in range(n_row):
            block = same if step % 2 == 0 else across
            if step:
                block = lax.ppermute(block, "row", [(r, (r + step) % n_row) for r in range(n_row)])
            blocks.append(block)
        targets.append(prepare_target(row, blocks, enc_rows))

    scale = 1.0 / jnp.sqrt(jnp.float32(src_count * n_row))
    recon_part = None
    for k in range(CHUNKS):
        partial = None
        for gathered, mask in sources:
            rows = chunk // tile
            term = partial_pre(gathered, targets[k], mask[None, k * rows : (k + 1) * rows], dec_rows, src_rows, norm)
            partial = term if partial is None else partial + term
        total = lax.dynamic_slice_in_dim(partial, group * piece, piece, 0)
        for step in range(1, members):
            target = lax.rem(group + step, members)
            sent = lax.dynamic_slice_in_dim(partial, target * piece, piece, 0)
            arrived = lax.ppermute(sent, "row", [(r, (r + 2 * step) % n_row) for r in range(n_row)])
            total = total + arrived
        bias = lax.dynamic_slice_in_dim(enc_bias, parity * half + k * chunk + group * piece, piece, 0)
        hidden = jnp.maximum(total * scale + bias[:, None], 0.0)
        hidden_all = lax.all_gather(hidden, "row", axis=0, tiled=True)
        starts = [(r % 2) * half + k * chunk + (r // 2) * piece for r in range(n_row)]
        dec_part = jnp.concatenate([dec_tgt[:, s : s + piece] for s in starts], axis=1)
        term = lax.dot_general(
            hidden_all, dec_part, (((0,), (1,)), ((), ())),
            precision=lax.Precision.HIGH, preferred_element_type=jnp.float32,
        )
        recon_part = term if recon_part is None else recon_part + term
    return lax.psum_scatter(recon_part, "col", scatter_dimension=0, tiled=True)


MESH = pl.DeviceIdType.MESH
T_CHUNKS = 4
S_CHUNKS = 4
X, Y, CORE = 2, 4, 1
HOPS = (
    (0, "all", X), (0, "all", Y), (0, "all", CORE),
    (X, "all", CORE), (Y, "all", CORE),
    (X, "top", Y), (Y, "low", X),
    (X ^ Y, "top", CORE), (X ^ Y, "low", CORE),
)


def fused(sizes, dec_src, src_coacts, eval_src, enc_tgt, tgt_coacts, masks, bias, dec_tgt, out, sbuf, tbuf, *scratch):
    n_row, n_col, dec_rows, src_rows, enc_rows, norm, scale = sizes
    (tstage, encs, tgts, stage, mask, acc, arrived, hidden, decoder, recon, rsend, rrecv, rsum, rlast,
     t_send, t_recv, s_send, s_recv, m_send, m_recv, x_send, x_recv, p_send, p_recv, h_send, h_recv,
     r_send, r_recv, local_sem, load_sem) = scratch
    r, c = lax.axis_index("row"), lax.axis_index("col")
    parity = lax.rem(r, 2)
    count = dec_src.shape[1]
    jw = count // S_CHUNKS
    half = enc_tgt.shape[1] // 2
    w = half // T_CHUNKS
    packed_rows = dec_rows + src_rows + eval_src.shape[0]

    def row_of(step):
        return lax.rem(r + step, n_row)

    def remote(src, dst, send, recv, row, col):
        return pltpu.make_async_remote_copy(
            src_ref=src, dst_ref=dst, send_sem=send, recv_sem=recv, device_id=(row, col), device_id_type=MESH
        )

    def t_cols(side, k):
        return pl.ds(pl.multiple_of(side * half + k * w, w), w)

    def t_start(k, step):
        to = row_of(step)
        start = 0
        for a in (enc_tgt, tgt_coacts):
            rows = pl.ds(start, a.shape[0])
            start += a.shape[0]
            remote(
                a.at[:, t_cols(lax.rem(to, 2), k)], tbuf.at[k, r, rows],
                t_send.at[k, step - 1], t_recv.at[k, step - 1], to, c,
            ).start()

    def t_whole(k, step):
        slot = tbuf.at[k, row_of(n_row - step)]
        return remote(slot, slot, t_send.at[k, step - 1], t_recv.at[k, step - 1], row_of(step), c)

    def s_cols(j):
        return pl.ds(pl.multiple_of(j * jw, jw), jw)

    def packed(j, dst):
        start = 0
        for a in (dec_src, src_coacts, eval_src):
            rows = pl.ds(start, a.shape[0])
            start += a.shape[0]
            yield a.at[:, s_cols(j)], dst(rows)

    def s_start(j):
        for src, dst in packed(j, lambda rows: sbuf.at[1, c, rows, s_cols(j)]):
            remote(src, dst, s_send.at[j], s_recv.at[j], r ^ 1, c).start()

    def s_copy(j):
        whole_chunk = sbuf.at[1, c, :, s_cols(j)]
        return remote(whole_chunk, whole_chunk, s_send.at[j], s_recv.at[j], r ^ 1, c)

    def m_copy():
        return remote(masks.at[1 - parity], mask.at[1], m_send, m_recv, r ^ 1, c)

    parts = {
        "all": pl.ds(0, packed_rows),
        "top": pl.ds(0, packed_rows // 2),
        "low": pl.ds(packed_rows // 2, packed_rows - packed_rows // 2),
    }

    def hop(q, n):
        whose, rows, to = HOPS[n]
        block, j = q // S_CHUNKS, q % S_CHUNKS
        dst = sbuf.at[block, c ^ whose, parts[rows], s_cols(j)]
        return remote(dst, dst, x_send.at[q, n], x_recv.at[q, n], r, c ^ to)

    def hop_wait(q, n):
        whose, rows, to = HOPS[n]
        block, j = q // S_CHUNKS, q % S_CHUNKS
        dst = sbuf.at[block, c ^ whose ^ to, parts[rows], s_cols(j)]
        remote(dst, dst, x_send.at[q, n], x_recv.at[q, n], r, c ^ to).wait_recv()

    chunks = 2 * S_CHUNKS

    def spread(q):
        if q >= S_CHUNKS:
            s_copy(q - S_CHUNKS).wait_recv()
        for n in (0, 1, 2):
            if q >= S_CHUNKS:
                hop(q, n).start()
            else:
                for src, dst in packed(q, lambda rows: sbuf.at[0, c, rows, s_cols(q)]):
                    remote(src, dst, x_send.at[q, n], x_recv.at[q, n], r, c ^ HOPS[n][2]).start()

    def step(q):
        if q < chunks:
            hop_wait(q, 0)
            hop(q, 5).start()
            hop(q, 3).start()
            hop_wait(q, 1)
            hop(q, 6).start()
            hop(q, 4).start()
        if q + 2 < chunks:
            spread(q + 2)
        if q >= 1:
            hop_wait(q - 1, 5)
            hop(q - 1, 7).start()
            hop_wait(q - 1, 6)
            hop(q - 1, 8).start()

    def landed(q):
        for n in (2, 3, 4, 7, 8):
            hop_wait(q, n)

    def load(block, j, slot, i):
        s = c ^ i
        return pltpu.make_async_copy(sbuf.at[block, s, :, s_cols(j)], stage.at[slot, s], load_sem.at[slot, i])

    def load_start(block, j, slot):
        @pl.when(block == 0)
        def _():
            for src, dst in packed(j, lambda rows: stage.at[slot, c, rows]):
                pltpu.make_async_copy(src, dst, load_sem.at[slot, 0]).start()

        @pl.when(block != 0)
        def _():
            load(block, j, slot, 0).start()

        for i in range(1, n_col):
            load(block, j, slot, i).start()

    def load_wait(slot):
        for i in range(n_col):
            load(0, 0, slot, i).wait()

    def prepare_chunk(k):
        for s in range(1, n_row):
            t_whole(k, s).wait_recv()
        start = 0
        for a in (enc_tgt, tgt_coacts):
            rows = pl.ds(start, a.shape[0])
            start += a.shape[0]
            pltpu.make_async_copy(a.at[:, t_cols(parity, k)], tstage.at[r, rows], local_sem.at[0]).start()
        copies = [
            pltpu.make_async_copy(tbuf.at[k, row_of(s)], tstage.at[row_of(s)], local_sem.at[s]) for s in range(n_row)
        ]
        for copy in copies[1:]:
            copy.start()
        for copy in copies:
            copy.wait()
        for rows, into in ((slice(None, enc_rows), encs), (slice(enc_rows, None), tgts)):
            into[k, :w], into[k, w:] = split(tstage[:, rows, :].reshape(-1, w).T)

    def compute(k, block, j, slot):
        dec = split(stage[slot, :, :dec_rows, :].reshape(-1, jw))
        virtual = dot3(encs[k], w, dec, 1, 0)
        src = split(stage[slot, :, dec_rows : dec_rows + src_rows, :].reshape(-1, jw))
        coact = dot3(tgts[k], w, src, 1, 0) * norm
        keep = mask[block, k, :, s_cols(j)]
        tiles = keep.shape[0]
        keep = jnp.broadcast_to(keep[:, None, :], (tiles, w // tiles, jw)).reshape(w, jw)
        weighted = jnp.concatenate(split(virtual * coact * keep), axis=0)
        evals = split(stage[slot, :, dec_rows + src_rows :, :].reshape(-1, jw))
        acc[k] += dot3(weighted, w, evals, 1, 1)

    def p_copy(k):
        return remote(acc.at[k], arrived.at[k], p_send.at[k], p_recv.at[k], r ^ 2, c)

    def h_copy(k, side):
        return remote(hidden.at[side, k], hidden.at[side, k], h_send.at[k], h_recv.at[k], r ^ 1, c)

    def activate(k):
        p_copy(k).wait_recv()
        column = jnp.broadcast_to(bias[pl.ds(parity * T_CHUNKS + k, 1), :], (128, w)).T[:, :1]
        hidden[parity, k] = jnp.maximum((acc[k] + arrived[k]) * scale + column, 0.0)
        h_copy(k, parity).start()

    def decode(k):
        h_copy(k, 1 - parity).wait_recv()
        for side in range(2):
            left = jnp.concatenate(split(decoder[:, t_cols(side, k)]), axis=0)
            recon[...] += dot3(left, decoder.shape[0], split(hidden[side, k]), 1, 0)

    def piece(i):
        rows = rsend.shape[0] // n_col
        return pl.ds(pl.multiple_of((c ^ i) * rows, rows), rows)

    def pair_copy(i):
        return remote(
            rsend.at[piece(i ^ CORE)], rrecv.at[c ^ i ^ CORE], r_send.at[i ^ CORE], r_recv.at[i ^ CORE], r, c ^ CORE
        )

    def pair_sum(i):
        slot = rrecv.at[c ^ i]
        remote(slot, slot, r_send.at[i ^ CORE], r_recv.at[i ^ CORE], r, c ^ CORE).wait_recv()
        return rsend[piece(i), :] + rrecv[c ^ i]

    def scatter_copy(i):
        return remote(rsum.at[c ^ i], rlast.at[c], r_send.at[i], r_recv.at[i], r, c ^ i)

    def scatter_wait(i):
        slot = rlast.at[c ^ i]
        remote(slot, slot, r_send.at[i], r_recv.at[i], r, c ^ i).wait_recv()

    barrier = pltpu.get_barrier_semaphore()
    for s in range(1, n_row):
        pl.semaphore_signal(barrier, inc=1, device_id=(row_of(s), c), device_id_type=MESH)
    for i in range(1, n_col):
        pl.semaphore_signal(barrier, inc=1, device_id=(r, c ^ i), device_id_type=MESH)
    pl.semaphore_wait(barrier, n_row + n_col - 2)

    m_copy().start()
    for s in range(1, n_row):
        t_start(0, s)
    spread(0)
    for j in range(S_CHUNKS):
        s_start(j)
    spread(1)
    for k in range(1, T_CHUNKS):
        for s in range(1, n_row):
            t_start(k, s)
    own_mask = pltpu.make_async_copy(masks.at[parity], mask.at[0], local_sem.at[n_row])
    own_mask.start()
    own_decoder = pltpu.make_async_copy(dec_tgt, decoder, local_sem.at[n_row + 1])
    own_decoder.start()
    acc[...] = jnp.zeros_like(acc)
    recon[...] = jnp.zeros_like(recon)
    step(0)
    step(1)
    own_mask.wait()
    own_decoder.wait()
    m_copy().wait_recv()

    def where(g):
        k = jnp.where(g < 6, 0, jnp.where(g < 12, 1, jnp.where(g < 16, g % 2, g // 8)))
        block = jnp.where(
            g < 4, 0, jnp.where(g < 6, 1, jnp.where(g < 10, 0, jnp.where(g < 16, 1, (g // 4) % 2)))
        )
        j = jnp.where(
            g < 4, g, jnp.where(g < 6, g - 4, jnp.where(g < 10, g - 6, jnp.where(g < 12, g - 10, jnp.where(g < 16, 2 + (g - 12) // 2, g % 4))))
        )
        return k, block, j

    needs = {0: 0, 1: 1, 2: 2, 3: 3, 4: 4, 5: 5, 12: 6, 14: 7}
    steps = {1: 2, 2: 3, 3: 4, 4: 5, 5: 6, 12: 7, 14: 8}

    @pl.loop(0, T_CHUNKS * chunks)
    def _(g):
        k, block, j = where(g)
        slot = g % 2
        for at, q in needs.items():
            @pl.when(g == at)
            def _(at=at, q=q):
                if at in steps:
                    step(steps[at])
                landed(q)

        waits = functools.reduce(jnp.logical_or, [g == at for at in needs])
        next_waits = functools.reduce(jnp.logical_or, [g + 1 == at for at in needs])

        @pl.when(waits)
        def _():
            load_start(block, j, slot)

        @pl.when((g == 0) | (g == 6) | (g == 16) | (g == 24))
        def _():
            prepare_chunk(k)

        @pl.when(jnp.logical_not(next_waits) & (g + 1 < T_CHUNKS * chunks))
        def _():
            load_start(*where(g + 1)[1:], 1 - slot)

        load_wait(slot)
        compute(k, block, j, slot)

        @pl.when((g == 14) | (g == 15) | (g == 23) | (g == 31))
        def _():
            p_copy(k).start()

        @pl.when((g == 27) | (g == 28) | (g == 30))
        def _():
            activate(jnp.where(g == 30, 2, g - 27))

    for k in range(T_CHUNKS):
        if k == T_CHUNKS - 1:
            activate(k)
        decode(k)
    rsend[...] = recon[...].T
    chips = (X ^ Y, X, Y)
    for i in chips + (0,):
        pair_copy(i).start()
    for i in chips:
        rsum[c ^ i] = pair_sum(i)
        scatter_copy(i).start()
    total = pair_sum(0)
    for i in chips:
        scatter_wait(i)
        total = total + rlast[c ^ i]
    out[...] = total

    m_copy().wait_send()
    for j in range(S_CHUNKS):
        s_copy(j).wait_send()
    for k in range(T_CHUNKS):
        for s in range(1, n_row):
            t_whole(k, s).wait_send()
        p_copy(k).wait_send()
        h_copy(k, parity).wait_send()
    for q in range(chunks):
        for n in range(len(HOPS)):
            hop(q, n).wait_send()
    for i in chips + (0,):
        pair_copy(i).wait_send()
    for i in chips:
        scatter_copy(i).wait_send()


def whole(n_row, n_col, dec_src, enc_tgt, src_coacts, tgt_coacts, eval_src, enc_bias, dec_tgt, tile_mask):
    count, features = dec_src.shape[1], enc_tgt.shape[1]
    dec_rows, src_rows, ev_rows = dec_src.shape[0], src_coacts.shape[0], eval_src.shape[0]
    enc_rows, tgt_rows = enc_tgt.shape[0], tgt_coacts.shape[0]
    half = features // 2
    w = half // T_CHUNKS
    jw = count // S_CHUNKS
    packed_rows, block_rows = dec_rows + src_rows + ev_rows, enc_rows + tgt_rows
    tile = count // tile_mask.shape[0]
    masks = jnp.repeat(tile_mask.T.astype(jnp.float32), tile, axis=1).reshape(2, T_CHUNKS, w // tile, count)
    sizes = (
        n_row, n_col, dec_rows, src_rows, enc_rows,
        1.0 / float(tgt_rows * n_row) ** 0.5, 1.0 / float(count * n_row) ** 0.5,
    )
    evals = ev_rows * n_col
    depth, stats = dec_rows * n_col, src_rows * n_col
    anywhere, vmem = pl.BlockSpec(memory_space=pl.ANY), pl.BlockSpec(memory_space=pltpu.VMEM)
    dma = pltpu.SemaphoreType.DMA
    f32, bf16 = jnp.float32, jnp.bfloat16
    hops = (2 * S_CHUNKS, len(HOPS))
    outs = pl.pallas_call(
        functools.partial(fused, sizes),
        in_specs=[anywhere] * 6 + [vmem, anywhere],
        out_specs=[vmem, anywhere, anywhere],
        out_shape=[
            jax.ShapeDtypeStruct((ev_rows, dec_tgt.shape[0]), f32),
            jax.ShapeDtypeStruct((2, n_col, packed_rows, count), f32),
            jax.ShapeDtypeStruct((T_CHUNKS, n_row, block_rows, w), f32),
        ],
        scratch_shapes=[
            pltpu.VMEM((n_row, block_rows, w), f32),
            pltpu.VMEM((T_CHUNKS, 2 * w, depth), bf16),
            pltpu.VMEM((T_CHUNKS, 2 * w, stats), bf16),
            pltpu.VMEM((2, n_col, packed_rows, jw), f32),
            pltpu.VMEM((2,) + masks.shape[1:], f32),
            pltpu.VMEM((T_CHUNKS, w, evals), f32),
            pltpu.VMEM((T_CHUNKS, w, evals), f32),
            pltpu.VMEM((2, T_CHUNKS, w, evals), f32),
            pltpu.VMEM(dec_tgt.shape, f32),
            pltpu.VMEM((dec_tgt.shape[0], evals), f32),
            pltpu.VMEM((evals, dec_tgt.shape[0]), f32),
            pltpu.VMEM((n_col, ev_rows, dec_tgt.shape[0]), f32),
            pltpu.VMEM((n_col, ev_rows, dec_tgt.shape[0]), f32),
            pltpu.VMEM((n_col, ev_rows, dec_tgt.shape[0]), f32),
            dma((T_CHUNKS, n_row - 1)), dma((T_CHUNKS, n_row - 1)),
            dma((S_CHUNKS,)), dma((S_CHUNKS,)),
            dma(()), dma(()),
            dma(hops), dma(hops),
            dma((T_CHUNKS,)), dma((T_CHUNKS,)),
            dma((T_CHUNKS,)), dma((T_CHUNKS,)),
            dma((n_col,)), dma((n_col,)),
            dma((n_row + 2,)), dma((2, n_col)),
        ],
        compiler_params=pltpu.CompilerParams(
            collective_id=0, has_side_effects=True, vmem_limit_bytes=VMEM_LIMIT
        ),
    )(dec_src, src_coacts, eval_src, enc_tgt, tgt_coacts, masks, enc_bias.reshape(-1, w), dec_tgt)
    return outs[0]


VMEM_LIMIT = 67000000


def solution(mesh):
    n_row, n_col = mesh.shape["row"], mesh.shape["col"]
    if (n_row, n_col) == (4, 8):
        return jax.shard_map(
            functools.partial(whole, n_row, n_col), mesh=mesh, in_specs=SPECS, out_specs=P("col", "row"), check_vma=False
        )
    return stepwise(mesh)


SPECS = (
    P("col", "row"), P("row", "col"), P("col", "row"), P("row", "col"),
    P("col", "row"), P("col"), P("row", "col"), P("row", "col"),
)


def stepwise(mesh):
    return jax.shard_map(
        functools.partial(layer, mesh.shape["row"]),
        mesh=mesh,
        in_specs=(
            P("col", "row"),
            P("row", "col"),
            P("col", "row"),
            P("row", "col"),
            P("col", "row"),
            P("col"),
            P("row", "col"),
            P("row", "col"),
        ),
        out_specs=P("col", "row"),
        check_vma=False,
    )
```

```python
import functools

import jax
import jax.numpy as jnp
from jax import lax
from jax.experimental import pallas as pl
from jax.experimental.pallas import tpu as pltpu
from jax.sharding import PartitionSpec as P


CHUNKS = 2


def split(value):
    high = value.astype(jnp.bfloat16)
    return high, (value - high.astype(jnp.float32)).astype(jnp.bfloat16)


def dot3(left, rows, right, left_dim, right_dim):
    def one(a, b):
        return lax.dot_general(a, b, (((left_dim,), (right_dim,)), ((), ())), preferred_element_type=jnp.float32)

    both = one(left, right[0])
    return both[:rows] + (both[rows:] + one(left[:rows], right[1]))


def prepare(enc_rows, row, *refs):
    blocks, (enc_both, tgt_both, ordered) = refs[:-3], refs[-3:]
    n_row, height = len(blocks), ordered.shape[2]
    for step, block in enumerate(blocks):
        ordered[lax.rem(row[0] + n_row - step, n_row)] = block[...]
    for rows, out in ((slice(None, enc_rows), enc_both), (slice(enc_rows, None), tgt_both)):
        out[:height], out[height:] = split(ordered[:, rows, :].reshape(-1, height).T)


def prepare_target(row, blocks, enc_rows):
    n_row = len(blocks)
    rows, height = blocks[0].shape
    shapes = [(2 * height, n_row * n) for n in (enc_rows, rows - enc_rows)]
    return pl.pallas_call(
        functools.partial(prepare, enc_rows),
        in_specs=[pl.BlockSpec(memory_space=pltpu.SMEM)] + [pl.BlockSpec(memory_space=pltpu.VMEM)] * n_row,
        out_specs=[pl.BlockSpec(memory_space=pltpu.VMEM)] * 2,
        out_shape=[jax.ShapeDtypeStruct(shape, jnp.bfloat16) for shape in shapes],
        scratch_shapes=[pltpu.VMEM((n_row, rows, height), jnp.float32)],
        compiler_params=pltpu.CompilerParams(vmem_limit_bytes=60 * 1024 * 1024),
        cost_estimate=pl.CostEstimate(flops=0, bytes_accessed=8 * n_row * rows * height, transcendentals=0),
    )(row.reshape(1), *blocks)


def weigh(dec_rows, src_rows, norm, source, enc_both, tgt_both, mask, out):
    width = source.shape[2]
    height = out.shape[0]

    @pl.when(pl.program_id(0) == 0)
    def _():
        out[...] = jnp.zeros_like(out)

    dec = split(source[:, :dec_rows, :].reshape(-1, width))
    virtual = dot3(enc_both[...], height, dec, 1, 0)
    src = split(source[:, dec_rows : dec_rows + src_rows, :].reshape(-1, width))
    coact = dot3(tgt_both[...], height, src, 1, 0) * norm
    tiles = mask.shape[1]
    keep = jnp.broadcast_to(mask[0][:, None, :], (tiles, height // tiles, width)).reshape(height, width)
    weighted = jnp.concatenate(split(virtual * coact * keep), axis=0)
    evals = split(source[:, dec_rows + src_rows :, :].reshape(-1, width))
    out[...] += dot3(weighted, height, evals, 1, 1)


def partial_pre(source, target, mask, dec_rows, src_rows, norm):
    n_col, packed, count = source.shape
    height = target[0].shape[0] // 2
    depth, stats = target[0].shape[1], target[1].shape[1]
    width = min(256, count)
    evals = n_col * (packed - dec_rows - src_rows)
    return pl.pallas_call(
        functools.partial(weigh, dec_rows, src_rows, norm),
        grid=(count // width,),
        in_specs=[
            pl.BlockSpec((n_col, packed, width), lambda i: (0, 0, i)),
            pl.BlockSpec(target[0].shape, lambda i: (0, 0)),
            pl.BlockSpec(target[1].shape, lambda i: (0, 0)),
            pl.BlockSpec((1, mask.shape[1], width), lambda i: (0, 0, i)),
        ],
        out_specs=pl.BlockSpec((height, evals), lambda i: (0, 0)),
        out_shape=jax.ShapeDtypeStruct((height, evals), jnp.float32),
        compiler_params=pltpu.CompilerParams(vmem_limit_bytes=60 * 1024 * 1024),
        cost_estimate=pl.CostEstimate(
            flops=6 * count * height * (depth + stats + evals),
            bytes_accessed=4 * (source.size + height * (depth + stats)),
            transcendentals=0,
        ),
    )(source, *target, mask)


def layer(n_row, dec_src, enc_tgt, src_coacts, tgt_coacts, eval_src, enc_bias, dec_tgt, tile_mask):
    members = n_row // 2
    src_count = dec_src.shape[1]
    half = enc_tgt.shape[1] // 2
    chunk = half // CHUNKS
    piece = chunk // members
    dec_rows, src_rows, enc_rows = dec_src.shape[0], src_coacts.shape[0], enc_tgt.shape[0]
    stats = tgt_coacts.shape[0] * n_row
    tile = src_count // tile_mask.shape[0]
    row = lax.axis_index("row")
    parity = lax.rem(row, 2)
    group = row // 2
    norm = 1.0 / float(stats) ** 0.5

    packed = jnp.concatenate([dec_src, src_coacts, eval_src], axis=0)
    packed_other = lax.ppermute(packed, "row", [(r, r ^ 1) for r in range(n_row)])
    mask_t = tile_mask.T.astype(jnp.float32)
    mask_here = lax.dynamic_slice_in_dim(mask_t, parity * (half // tile), half // tile, 0)
    mask_there = lax.dynamic_slice_in_dim(mask_t, (1 - parity) * (half // tile), half // tile, 0)
    mask_other = lax.ppermute(mask_there, "row", [(r, r ^ 1) for r in range(n_row)])

    sources = [(lax.all_gather(packed, "col", axis=0, tiled=False), jnp.repeat(mask_here, tile, axis=1))]
    gathered = lax.all_gather(packed_other, "col", axis=0, tiled=False)
    sources.append((gathered, jnp.repeat(mask_other, tile, axis=1)))

    targets = []
    for k in range(CHUNKS):
        def columns(side):
            start = side * half + k * chunk
            return jnp.concatenate(
                [lax.dynamic_slice_in_dim(a, start, chunk, 1) for a in (enc_tgt, tgt_coacts)], axis=0
            )

        same, across = columns(parity), columns(1 - parity)
        blocks = []
        for step in range(n_row):
            block = same if step % 2 == 0 else across
            if step:
                block = lax.ppermute(block, "row", [(r, (r + step) % n_row) for r in range(n_row)])
            blocks.append(block)
        targets.append(prepare_target(row, blocks, enc_rows))

    scale = 1.0 / jnp.sqrt(jnp.float32(src_count * n_row))
    recon_part = None
    for k in range(CHUNKS):
        partial = None
        for gathered, mask in sources:
            rows = chunk // tile
            term = partial_pre(gathered, targets[k], mask[None, k * rows : (k + 1) * rows], dec_rows, src_rows, norm)
            partial = term if partial is None else partial + term
        total = lax.dynamic_slice_in_dim(partial, group * piece, piece, 0)
        for step in range(1, members):
            target = lax.rem(group + step, members)
            sent = lax.dynamic_slice_in_dim(partial, target * piece, piece, 0)
            arrived = lax.ppermute(sent, "row", [(r, (r + 2 * step) % n_row) for r in range(n_row)])
            total = total + arrived
        bias = lax.dynamic_slice_in_dim(enc_bias, parity * half + k * chunk + group * piece, piece, 0)
        hidden = jnp.maximum(total * scale + bias[:, None], 0.0)
        hidden_all = lax.all_gather(hidden, "row", axis=0, tiled=True)
        starts = [(r % 2) * half + k * chunk + (r // 2) * piece for r in range(n_row)]
        dec_part = jnp.concatenate([dec_tgt[:, s : s + piece] for s in starts], axis=1)
        term = lax.dot_general(
            hidden_all, dec_part, (((0,), (1,)), ((), ())),
            precision=lax.Precision.HIGH, preferred_element_type=jnp.float32,
        )
        recon_part = term if recon_part is None else recon_part + term
    return lax.psum_scatter(recon_part, "col", scatter_dimension=0, tiled=True)


MESH = pl.DeviceIdType.MESH
T_CHUNKS = 4
S_CHUNKS = 4
BANDS = 2
X, Y, CORE = 2, 4, 1
HOPS = (
    (0, "all", X), (0, "all", Y), (0, "all", CORE),
    (X, "all", CORE), (Y, "all", CORE),
    (X, "top", Y), (Y, "low", X),
    (X ^ Y, "top", CORE), (X ^ Y, "low", CORE),
)


def fused(sizes, dec_src, src_coacts, eval_src, enc_tgt, tgt_coacts, masks, bias, dec_tgt, out, sbuf, tbuf, *scratch):
    n_row, n_col, dec_rows, src_rows, enc_rows, norm, scale = sizes
    (tstage, encs, tgts, stage, mask, acc, arrived, hidden, decoder, recon, rsend, rrecv, rsum, rlast,
     t_send, t_recv, s_send, s_recv, m_send, m_recv, x_send, x_recv, p_send, p_recv, h_send, h_recv,
     r_send, r_recv, local_sem, load_sem) = scratch
    r, c = lax.axis_index("row"), lax.axis_index("col")
    parity = lax.rem(r, 2)
    count = dec_src.shape[1]
    jw = count // S_CHUNKS
    half = enc_tgt.shape[1] // 2
    w = half // T_CHUNKS
    packed_rows = dec_rows + src_rows + eval_src.shape[0]

    def row_of(step):
        return lax.rem(r + step, n_row)

    def remote(src, dst, send, recv, row, col):
        return pltpu.make_async_remote_copy(
            src_ref=src, dst_ref=dst, send_sem=send, recv_sem=recv, device_id=(row, col), device_id_type=MESH
        )

    def t_cols(side, k):
        return pl.ds(pl.multiple_of(side * half + k * w, w), w)

    def t_start(k, step):
        to = row_of(step)
        start = 0
        for a in (enc_tgt, tgt_coacts):
            rows = pl.ds(start, a.shape[0])
            start += a.shape[0]
            remote(
                a.at[:, t_cols(lax.rem(to, 2), k)], tbuf.at[k, r, rows],
                t_send.at[k, step - 1], t_recv.at[k, step - 1], to, c,
            ).start()

    def t_whole(k, step):
        slot = tbuf.at[k, row_of(n_row - step)]
        return remote(slot, slot, t_send.at[k, step - 1], t_recv.at[k, step - 1], row_of(step), c)

    def s_cols(j):
        return pl.ds(pl.multiple_of(j * jw, jw), jw)

    def packed(j, dst):
        start = 0
        for a in (dec_src, src_coacts, eval_src):
            rows = pl.ds(start, a.shape[0])
            start += a.shape[0]
            yield a.at[:, s_cols(j)], dst(rows)

    def s_start(j):
        for src, dst in packed(j, lambda rows: sbuf.at[1, c, rows, s_cols(j)]):
            remote(src, dst, s_send.at[j], s_recv.at[j], r ^ 1, c).start()

    def s_copy(j):
        whole_chunk = sbuf.at[1, c, :, s_cols(j)]
        return remote(whole_chunk, whole_chunk, s_send.at[j], s_recv.at[j], r ^ 1, c)

    def m_copy():
        return remote(masks.at[1 - parity], mask.at[1], m_send, m_recv, r ^ 1, c)

    parts = {
        "all": pl.ds(0, packed_rows),
        "top": pl.ds(0, packed_rows // 2),
        "low": pl.ds(packed_rows // 2, packed_rows - packed_rows // 2),
    }

    def hop(q, n):
        whose, rows, to = HOPS[n]
        block, j = q // S_CHUNKS, q % S_CHUNKS
        dst = sbuf.at[block, c ^ whose, parts[rows], s_cols(j)]
        return remote(dst, dst, x_send.at[q, n], x_recv.at[q, n], r, c ^ to)

    def hop_wait(q, n):
        whose, rows, to = HOPS[n]
        block, j = q // S_CHUNKS, q % S_CHUNKS
        dst = sbuf.at[block, c ^ whose ^ to, parts[rows], s_cols(j)]
        remote(dst, dst, x_send.at[q, n], x_recv.at[q, n], r, c ^ to).wait_recv()

    chunks = 2 * S_CHUNKS

    def spread(q):
        if q >= S_CHUNKS:
            s_copy(q - S_CHUNKS).wait_recv()
        for n in (0, 1, 2):
            if q >= S_CHUNKS:
                hop(q, n).start()
            else:
                for src, dst in packed(q, lambda rows: sbuf.at[0, c, rows, s_cols(q)]):
                    remote(src, dst, x_send.at[q, n], x_recv.at[q, n], r, c ^ HOPS[n][2]).start()

    def step(q):
        if q < chunks:
            hop_wait(q, 0)
            hop(q, 5).start()
            hop(q, 3).start()
            hop_wait(q, 1)
            hop(q, 6).start()
            hop(q, 4).start()
        if q + 2 < chunks:
            spread(q + 2)
        if q >= 1:
            hop_wait(q - 1, 5)
            hop(q - 1, 7).start()
            hop_wait(q - 1, 6)
            hop(q - 1, 8).start()

    def landed(q):
        for n in (2, 3, 4, 7, 8):
            hop_wait(q, n)

    def load(block, j, slot, i):
        s = c ^ i
        return pltpu.make_async_copy(sbuf.at[block, s, :, s_cols(j)], stage.at[slot, s], load_sem.at[slot, i])

    def load_start(block, j, slot):
        @pl.when(block == 0)
        def _():
            for src, dst in packed(j, lambda rows: stage.at[slot, c, rows]):
                pltpu.make_async_copy(src, dst, load_sem.at[slot, 0]).start()

        @pl.when(block != 0)
        def _():
            load(block, j, slot, 0).start()

        for i in range(1, n_col):
            load(block, j, slot, i).start()

    def load_wait(slot):
        for i in range(n_col):
            load(0, 0, slot, i).wait()

    def prepare_chunk(k):
        for s in range(1, n_row):
            t_whole(k, s).wait_recv()
        start = 0
        for a in (enc_tgt, tgt_coacts):
            rows = pl.ds(start, a.shape[0])
            start += a.shape[0]
            pltpu.make_async_copy(a.at[:, t_cols(parity, k)], tstage.at[r, rows], local_sem.at[0]).start()
        copies = [
            pltpu.make_async_copy(tbuf.at[k, row_of(s)], tstage.at[row_of(s)], local_sem.at[s]) for s in range(n_row)
        ]
        for copy in copies[1:]:
            copy.start()
        for copy in copies:
            copy.wait()
        for rows, into in ((slice(None, enc_rows), encs), (slice(enc_rows, None), tgts)):
            into[k, :w], into[k, w:] = split(tstage[:, rows, :].reshape(-1, w).T)

    def compute(k, block, j, slot):
        dec = split(stage[slot, :, :dec_rows, :].reshape(-1, jw))
        virtual = dot3(encs[k], w, dec, 1, 0)
        src = split(stage[slot, :, dec_rows : dec_rows + src_rows, :].reshape(-1, jw))
        coact = dot3(tgts[k], w, src, 1, 0) * norm
        keep = mask[block, k, :, s_cols(j)]
        tiles = keep.shape[0]
        keep = jnp.broadcast_to(keep[:, None, :], (tiles, w // tiles, jw)).reshape(w, jw)
        weighted = jnp.concatenate(split(virtual * coact * keep), axis=0)
        evals = split(stage[slot, :, dec_rows + src_rows :, :].reshape(-1, jw))
        acc[k] += dot3(weighted, w, evals, 1, 1)

    def bands():
        return [(b, pl.ds(b * (w // BANDS), w // BANDS)) for b in range(BANDS)]

    def p_copy(k, b, rows):
        return remote(acc.at[k, rows], arrived.at[k, rows], p_send.at[k, b], p_recv.at[k, b], r ^ 2, c)

    def h_copy(k, b, rows, side):
        part = hidden.at[side, k, rows]
        return remote(part, part, h_send.at[k, b], h_recv.at[k, b], r ^ 1, c)

    def activate(k):
        column = jnp.broadcast_to(bias[pl.ds(parity * T_CHUNKS + k, 1), :], (128, w)).T[:, :1]
        for b, rows in bands():
            p_copy(k, b, rows).wait_recv()
            total = (acc[k, rows, :] + arrived[k, rows, :]) * scale + column[b * (w // BANDS) : (b + 1) * (w // BANDS)]
            hidden[parity, k, rows, :] = jnp.maximum(total, 0.0)
            h_copy(k, b, rows, parity).start()

    def decode(k, side):
        left = jnp.concatenate(split(decoder[:, t_cols(side, k)]), axis=0)
        recon[...] += dot3(left, decoder.shape[0], split(hidden[side, k]), 1, 0)

    def piece(i):
        rows = rsend.shape[0] // n_col
        return pl.ds(pl.multiple_of((c ^ i) * rows, rows), rows)

    def pair_copy(i):
        return remote(
            rsend.at[piece(i ^ CORE)], rrecv.at[c ^ i ^ CORE], r_send.at[i ^ CORE], r_recv.at[i ^ CORE], r, c ^ CORE
        )

    def pair_sum(i):
        slot = rrecv.at[c ^ i]
        remote(slot, slot, r_send.at[i ^ CORE], r_recv.at[i ^ CORE], r, c ^ CORE).wait_recv()
        return rsend[piece(i), :] + rrecv[c ^ i]

    def scatter_copy(i):
        return remote(rsum.at[c ^ i], rlast.at[c], r_send.at[i], r_recv.at[i], r, c ^ i)

    def scatter_wait(i):
        slot = rlast.at[c ^ i]
        remote(slot, slot, r_send.at[i], r_recv.at[i], r, c ^ i).wait_recv()

    barrier = pltpu.get_barrier_semaphore()
    for s in range(1, n_row):
        pl.semaphore_signal(barrier, inc=1, device_id=(row_of(s), c), device_id_type=MESH)
    for i in range(1, n_col):
        pl.semaphore_signal(barrier, inc=1, device_id=(r, c ^ i), device_id_type=MESH)
    pl.semaphore_wait(barrier, n_row + n_col - 2)

    m_copy().start()
    for s in range(1, n_row):
        t_start(0, s)
    spread(0)
    for j in range(S_CHUNKS):
        s_start(j)
    spread(1)
    for k in range(1, T_CHUNKS):
        for s in range(1, n_row):
            t_start(k, s)
    own_mask = pltpu.make_async_copy(masks.at[parity], mask.at[0], local_sem.at[n_row])
    own_mask.start()
    own_decoder = pltpu.make_async_copy(dec_tgt, decoder, local_sem.at[n_row + 1])
    own_decoder.start()
    acc[...] = jnp.zeros_like(acc)
    recon[...] = jnp.zeros_like(recon)
    step(0)
    step(1)
    own_mask.wait()
    own_decoder.wait()
    m_copy().wait_recv()

    def where(g):
        k = jnp.where(g < 6, 0, jnp.where(g < 12, 1, jnp.where(g < 16, g % 2, g // 8)))
        block = jnp.where(
            g < 4, 0, jnp.where(g < 6, 1, jnp.where(g < 10, 0, jnp.where(g < 16, 1, (g // 4) % 2)))
        )
        j = jnp.where(
            g < 4, g, jnp.where(g < 6, g - 4, jnp.where(g < 10, g - 6, jnp.where(g < 12, g - 10, jnp.where(g < 16, 2 + (g - 12) // 2, g % 4))))
        )
        return k, block, j

    needs = {0: 0, 1: 1, 2: 2, 3: 3, 4: 4, 5: 5, 12: 6, 14: 7}
    steps = {1: 2, 2: 3, 3: 4, 4: 5, 5: 6, 12: 7, 14: 8}

    @pl.loop(0, T_CHUNKS * chunks)
    def _(g):
        k, block, j = where(g)
        slot = g % 2
        for at, q in needs.items():
            @pl.when(g == at)
            def _(at=at, q=q):
                if at in steps:
                    step(steps[at])
                landed(q)

        waits = functools.reduce(jnp.logical_or, [g == at for at in needs])
        next_waits = functools.reduce(jnp.logical_or, [g + 1 == at for at in needs])

        @pl.when(waits)
        def _():
            load_start(block, j, slot)

        @pl.when((g == 0) | (g == 6) | (g == 16) | (g == 24))
        def _():
            prepare_chunk(k)

        @pl.when(jnp.logical_not(next_waits) & (g + 1 < T_CHUNKS * chunks))
        def _():
            load_start(*where(g + 1)[1:], 1 - slot)

        load_wait(slot)
        compute(k, block, j, slot)

        @pl.when((g == 14) | (g == 15) | (g == 23) | (g == 31))
        def _():
            for b, rows in bands():
                p_copy(k, b, rows).start()

        @pl.when((g == 27) | (g == 28) | (g == 30))
        def _():
            activate(jnp.where(g == 30, 2, g - 27))

    last = T_CHUNKS - 1

    @pl.loop(0, last)
    def _(k):
        decode(k, parity)

    activate(last)
    decode(last, parity)

    @pl.loop(0, T_CHUNKS)
    def _(k):
        for b, rows in bands():
            h_copy(k, b, rows, 1 - parity).wait_recv()
        decode(k, 1 - parity)

    rsend[...] = recon[...].T
    chips = (X ^ Y, X, Y)
    for i in chips + (0,):
        pair_copy(i).start()
    for i in chips:
        rsum[c ^ i] = pair_sum(i)
        scatter_copy(i).start()
    total = pair_sum(0)
    for i in chips:
        scatter_wait(i)
        total = total + rlast[c ^ i]
    out[...] = total

    m_copy().wait_send()
    for j in range(S_CHUNKS):
        s_copy(j).wait_send()
    for k in range(T_CHUNKS):
        for s in range(1, n_row):
            t_whole(k, s).wait_send()
        for b, rows in bands():
            p_copy(k, b, rows).wait_send()
            h_copy(k, b, rows, parity).wait_send()
    for q in range(chunks):
        for n in range(len(HOPS)):
            hop(q, n).wait_send()
    for i in chips + (0,):
        pair_copy(i).wait_send()
    for i in chips:
        scatter_copy(i).wait_send()


def whole(n_row, n_col, dec_src, enc_tgt, src_coacts, tgt_coacts, eval_src, enc_bias, dec_tgt, tile_mask):
    count, features = dec_src.shape[1], enc_tgt.shape[1]
    dec_rows, src_rows, ev_rows = dec_src.shape[0], src_coacts.shape[0], eval_src.shape[0]
    enc_rows, tgt_rows = enc_tgt.shape[0], tgt_coacts.shape[0]
    half = features // 2
    w = half // T_CHUNKS
    jw = count // S_CHUNKS
    packed_rows, block_rows = dec_rows + src_rows + ev_rows, enc_rows + tgt_rows
    tile = count // tile_mask.shape[0]
    masks = jnp.repeat(tile_mask.T.astype(jnp.float32), tile, axis=1).reshape(2, T_CHUNKS, w // tile, count)
    sizes = (
        n_row, n_col, dec_rows, src_rows, enc_rows,
        1.0 / float(tgt_rows * n_row) ** 0.5, 1.0 / float(count * n_row) ** 0.5,
    )
    evals = ev_rows * n_col
    depth, stats = dec_rows * n_col, src_rows * n_col
    anywhere, vmem = pl.BlockSpec(memory_space=pl.ANY), pl.BlockSpec(memory_space=pltpu.VMEM)
    dma = pltpu.SemaphoreType.DMA
    f32, bf16 = jnp.float32, jnp.bfloat16
    hops = (2 * S_CHUNKS, len(HOPS))
    outs = pl.pallas_call(
        functools.partial(fused, sizes),
        in_specs=[anywhere] * 6 + [vmem, anywhere],
        out_specs=[vmem, anywhere, anywhere],
        out_shape=[
            jax.ShapeDtypeStruct((ev_rows, dec_tgt.shape[0]), f32),
            jax.ShapeDtypeStruct((2, n_col, packed_rows, count), f32),
            jax.ShapeDtypeStruct((T_CHUNKS, n_row, block_rows, w), f32),
        ],
        scratch_shapes=[
            pltpu.VMEM((n_row, block_rows, w), f32),
            pltpu.VMEM((T_CHUNKS, 2 * w, depth), bf16),
            pltpu.VMEM((T_CHUNKS, 2 * w, stats), bf16),
            pltpu.VMEM((2, n_col, packed_rows, jw), f32),
            pltpu.VMEM((2,) + masks.shape[1:], f32),
            pltpu.VMEM((T_CHUNKS, w, evals), f32),
            pltpu.VMEM((T_CHUNKS, w, evals), f32),
            pltpu.VMEM((2, T_CHUNKS, w, evals), f32),
            pltpu.VMEM(dec_tgt.shape, f32),
            pltpu.VMEM((dec_tgt.shape[0], evals), f32),
            pltpu.VMEM((evals, dec_tgt.shape[0]), f32),
            pltpu.VMEM((n_col, ev_rows, dec_tgt.shape[0]), f32),
            pltpu.VMEM((n_col, ev_rows, dec_tgt.shape[0]), f32),
            pltpu.VMEM((n_col, ev_rows, dec_tgt.shape[0]), f32),
            dma((T_CHUNKS, n_row - 1)), dma((T_CHUNKS, n_row - 1)),
            dma((S_CHUNKS,)), dma((S_CHUNKS,)),
            dma(()), dma(()),
            dma(hops), dma(hops),
            dma((T_CHUNKS, BANDS)), dma((T_CHUNKS, BANDS)),
            dma((T_CHUNKS, BANDS)), dma((T_CHUNKS, BANDS)),
            dma((n_col,)), dma((n_col,)),
            dma((n_row + 2,)), dma((2, n_col)),
        ],
        compiler_params=pltpu.CompilerParams(
            collective_id=0, has_side_effects=True, vmem_limit_bytes=VMEM_LIMIT
        ),
    )(dec_src, src_coacts, eval_src, enc_tgt, tgt_coacts, masks, enc_bias.reshape(-1, w), dec_tgt)
    return outs[0]


VMEM_LIMIT = 67000000


def solution(mesh):
    n_row, n_col = mesh.shape["row"], mesh.shape["col"]
    if (n_row, n_col) == (4, 8):
        return jax.shard_map(
            functools.partial(whole, n_row, n_col), mesh=mesh, in_specs=SPECS, out_specs=P("col", "row"), check_vma=False
        )
    return stepwise(mesh)


SPECS = (
    P("col", "row"), P("row", "col"), P("col", "row"), P("row", "col"),
    P("col", "row"), P("col"), P("row", "col"), P("row", "col"),
)


def stepwise(mesh):
    return jax.shard_map(
        functools.partial(layer, mesh.shape["row"]),
        mesh=mesh,
        in_specs=(
            P("col", "row"),
            P("row", "col"),
            P("col", "row"),
            P("row", "col"),
            P("col", "row"),
            P("col"),
            P("row", "col"),
            P("row", "col"),
        ),
        out_specs=P("col", "row"),
        check_vma=False,
    )
```
